32 devices in a mesh: blk: 4 (over y, core), rows: 8 (over z, x).
Axes of the slice: x: 2, y: 2, z: 4, core: 2. Of those that a mesh axis runs over, the one named last changes fastest.
Arguments:
- section_weights: bfloat16 [4, 256, 9, 256], P('blk'), may hold values from -0.125 to 0.125
- grad_acc: bfloat16 [4, 256, 9, 256], P('blk', 'rows'), may hold values from -6 to 6
- saved_inputs: bfloat16 [3, 4, 32, 256, 256], P(None, 'blk', 'rows'), may hold values from -6 to 6
- cotangent: bfloat16 [4, 32, 256, 256], P('blk', 'rows'), may hold values from -6 to 6
- fresh_grads: bfloat16 [2, 32, 256, 256], P(None, 'rows'), may hold values from -6 to 6
Outputs:
- tick_states: bfloat16 [3, 4, 32, 256, 256], P(None, 'blk', 'rows')
- grad_out: bfloat16 [4, 256, 9, 256], P('blk', 'rows')
The draws below stay inside these ranges and needn't reach their ends.
All inputs are finite; a program needn't handle non-finite values.
Results may differ from the reference program's by a relative error of at most 0.0057.
Values may be sent and summed in bfloat16 or wider, within the bound.
A program may use at most 128 MiB of HBM per device.

```python
import jax
import jax.numpy as jnp
from jax import lax

CH = 256
TICKS = 3
COLS = 256
LAYERS = 4
IMAGES = 4
HEIGHT = 32


def block_levels(own_key, extent, pieces, smallest, high):
    gain, own = 1.0, jax.random.fold_in(own_key, 6)
    for axis_at, shards_of in pieces:
        draws = jnp.exp(jax.random.uniform(jax.random.fold_in(own, axis_at), (shards_of,), jnp.float32, smallest / len(pieces), high / len(pieces)))
        gain = gain * jnp.repeat(draws, extent[axis_at] // shards_of).reshape([-1 if axis == axis_at else 1 for axis in range(len(extent))])
    return gain


def normal_values(rng, shape, deviation, reach, cuts=(), kind=jnp.bfloat16):
    factor_of = block_levels(rng, shape, cuts, -0.22, 0.18) if cuts else 1.0
    values = jax.random.normal(rng, shape, jnp.float32) * deviation * factor_of
    return jnp.minimum(jnp.maximum(values, -reach), reach).astype(kind)


def setup_inputs(seed: int = 0) -> dict:
    keys = jax.random.split(jax.random.key(seed), 6)
    section_weights = normal_values(keys[0], (LAYERS, CH, 9, CH), (9 * CH) ** -0.5, 0.125, ((0, 4),))
    grad_acc = normal_values(keys[1], (LAYERS, CH, 9, CH), 1.0, 6.0, ((0, 4), (1, 8)))
    saved_inputs = normal_values(keys[2], (TICKS, IMAGES, HEIGHT, CH, COLS), 1.0, 6.0, ((1, 4), (2, 8)))
    cotangent = normal_values(keys[3], (IMAGES, HEIGHT, CH, COLS), 1.0, 6.0, ((0, 4), (1, 8)))
    fresh_grads = normal_values(keys[4], (TICKS - 1, HEIGHT, CH, COLS), 1.0, 6.0, ((1, 8),))
    return {"section_weights": section_weights, "grad_acc": grad_acc, "saved_inputs": saved_inputs, "cotangent": cotangent, "fresh_grads": fresh_grads}


def image_step(members):
    grad_now, saved_now, kernel = members
    height = grad_now.shape[0]
    columns = grad_now.shape[2]
    cell_scale = (saved_inputs_cells(height, columns)) ** -0.5
    inputs = jnp.maximum(saved_now, 0).astype(jnp.bfloat16)
    grad_float = grad_now.astype(jnp.float32)
    grad_wide = jnp.pad(grad_float, ((1, 1), (0, 0), (1, 1)))
    input_wide = jnp.pad(inputs.astype(jnp.float32), ((1, 1), (0, 0), (1, 1)))
    kernel_wide = kernel.astype(jnp.float32)
    back_sum = jnp.zeros(grad_now.shape, jnp.float32)
    tap_list = []
    for tap_index in range(9):
        row_shift = tap_index // 3
        col_shift = tap_index % 3
        window = grad_wide[2 - row_shift:2 - row_shift + height, :, 2 - col_shift:2 - col_shift + columns]
        back_sum = back_sum + jnp.einsum("oi,row->riw", kernel_wide[:, tap_index, :], window)
        source = input_wide[row_shift:row_shift + height, :, col_shift:col_shift + columns]
        tap_list.append(jnp.einsum("row,riw->oi", grad_float, source) * cell_scale)
    new_grads = jnp.where(saved_now > 0, back_sum, 0.0).astype(jnp.bfloat16)
    return new_grads, jnp.stack(tap_list, axis=1)


def saved_inputs_cells(height, columns):
    return float(height * columns)


def reference(section_weights, grad_acc, saved_inputs, cotangent, fresh_grads):
    images = cotangent.shape[0]
    current = cotangent
    running = grad_acc
    outputs = []
    for tick_index in range(TICKS):
        if tick_index > 0:
            restart = jnp.arange(images) == (images - tick_index) % images
            current = jnp.where(restart[:, None, None, None], fresh_grads[tick_index - 1][None], current)
        kernels = jnp.roll(section_weights, -tick_index, axis=0)
        new_grads, weight_grads = lax.map(image_step, (current, saved_inputs[tick_index], kernels))
        running = (running.astype(jnp.float32) + jnp.roll(weight_grads, tick_index, axis=0)).astype(jnp.bfloat16)
        outputs.append(new_grads)
        current = new_grads
    return jnp.stack(outputs), jnp.roll(running, -(TICKS - 1), axis=0)
```

```python
import functools

import jax
import jax.numpy as jnp
from jax import lax
from jax.experimental import pallas as pl
from jax.experimental.pallas import tpu as pltpu
from jax.sharding import PartitionSpec as P

TICKS = 3
MESH = pl.DeviceIdType.MESH
F32 = jnp.float32
BF16 = jnp.bfloat16


LATE = {(0, 0): (0, 1, 2), (0, 1): (0, 1, 2), (1, 0): (), (1, 1): ()}


def halving(bits, t, core, a):
    return [*range(1, bits), 0] if a in LATE[t, core] else list(range(bits))


def place(bits, t, core, a, value):
    return sum(((value >> k) & 1) << (bits - 1 - at) for at, k in enumerate(halving(bits, t, core, a)))


def kernel(
    shape, w_hbm, acc_hbm, saved_hbm, cot_hbm, fresh_hbm, states_hbm, out_ref,
    kern, kern_t, sv, cur, fresh, xs, gs, halo, states, dk, rx, part, sib, held, held_rx,
    load_sem, halo_send, halo_recv, k_send, k_recv, rs_send, rs_recv, acc_send, acc_recv, sib_send, sib_recv, st_sem,
):
    peers, cycle, height, ch, cols, scale = shape
    bits = peers.bit_length() - 1
    row = lax.axis_index("rows")
    pos = lax.axis_index("blk")
    below = lax.rem(pos + cycle - 1, cycle)
    bit = [lax.rem(row // (1 << k), 2) for k in range(bits)]
    mate = [row + (1 - 2 * bit[k]) * (1 << k) for k in range(bits)]
    has_up = row > 0
    has_down = row < peers - 1
    restart = [None] + [pos == (cycle - t) % cycle for t in range(1, TICKS)]

    loads = [
        pltpu.make_async_copy(cot_hbm.at[0], cur.at[0], load_sem.at[0]),
        pltpu.make_async_copy(saved_hbm.at[0, 0], sv.at[0], load_sem.at[1]),
        pltpu.make_async_copy(w_hbm.at[0], kern.at[0], load_sem.at[2]),
        pltpu.make_async_copy(fresh_hbm, fresh, load_sem.at[3]),
        pltpu.make_async_copy(saved_hbm.at[1, 0], sv.at[1], load_sem.at[4]),
        pltpu.make_async_copy(saved_hbm.at[2, 0], sv.at[2], load_sem.at[5]),
        pltpu.make_async_copy(acc_hbm.at[0], held.at[0], load_sem.at[6]),
    ]
    for load in loads:
        load.start()

    barrier = pltpu.get_barrier_semaphore()
    core = lax.rem(pos, 2)
    sibling = pos + 1 - 2 * core
    far = lax.rem(pos + cycle - (TICKS - 1), cycle)
    hops = sorted({d % cycle for d in (1, -1, TICKS - 1, 1 - TICKS)})
    greet = [{"blk": lax.rem(pos + d, cycle)} for d in hops] + [{"rows": m} for m in mate]
    for who in greet:
        pl.semaphore_signal(barrier, inc=1, device_id=who, device_id_type=MESH)

    other = row + 2 * bit[0] - 1
    has_other = jnp.logical_and(other >= 0, other < peers)

    @pl.when(has_other)
    def _():
        pl.semaphore_signal(barrier, inc=1, device_id={"rows": other}, device_id_type=MESH)

    pl.semaphore_wait(barrier, len(greet) + has_other.astype(jnp.int32))

    def halo_copy(t, side):
        edge = 0 if side == 1 else height - 1
        return pltpu.make_async_remote_copy(
            src_ref=cur.at[t, edge],
            dst_ref=halo.at[t, side],
            send_sem=halo_send.at[t, side],
            recv_sem=halo_recv.at[t, side],
            device_id={"rows": row - 1 if side == 1 else row + 1},
            device_id_type=MESH,
        )

    def halo_start(t):
        @pl.when(has_up)
        def _():
            halo_copy(t, 1).start()

        @pl.when(has_down)
        def _():
            halo_copy(t, 0).start()

    def kern_copy(t):
        return pltpu.make_async_remote_copy(
            src_ref=kern.at[t],
            dst_ref=kern.at[t + 1],
            send_sem=k_send.at[t],
            recv_sem=k_recv.at[t],
            device_id={"blk": below},
            device_id_type=MESH,
        )

    held_copy = pltpu.make_async_remote_copy(
        src_ref=held.at[1],
        dst_ref=held_rx,
        send_sem=acc_send,
        recv_sem=acc_recv,
        device_id={"blk": far},
        device_id_type=MESH,
    )

    def sib_copy(a):
        return pltpu.make_async_remote_copy(
            src_ref=dk.at[1, a],
            dst_ref=sib.at[a],
            send_sem=sib_send.at[a],
            recv_sem=sib_recv.at[a],
            device_id={"blk": sibling},
            device_id_type=MESH,
        )

    wide = 3 * ch
    lane = lax.broadcasted_iota(jnp.int32, (ch, cols), 1)

    def put_row(index, value):
        base = pl.multiple_of(index * wide, wide)
        full = value.astype(F32)
        left = jnp.where(lane == cols - 1, 0.0, pltpu.roll(full, cols - 1, 1))
        right = jnp.where(lane == 0, 0.0, pltpu.roll(full, 1, 1))
        gs[pl.ds(base, ch), :] = left.astype(BF16)
        gs[pl.ds(base + ch, ch), :] = value
        gs[pl.ds(base + 2 * ch, ch), :] = right.astype(BF16)

    def inner_rows(t):
        def step(r, carry):
            put_row(r + 1, cur[t, r])
            return carry

        lax.fori_loop(0, height, step, 0)
        for r in range(height):
            xs[:, r * cols : (r + 1) * cols] = jnp.maximum(sv[t, r], 0)

    def outer_rows(t):
        for side, have, index in ((0, has_up, 0), (1, has_down, height + 1)):
            @pl.when(have)
            def _():
                halo_copy(t, side).wait_recv()
                put_row(index, halo[t, side])

            @pl.when(jnp.logical_not(have))
            def _():
                gs[index * wide : (index + 1) * wide, :] = jnp.zeros((wide, cols), BF16)

    def turn_kernel(t):
        for tap in range(9):
            a, b = tap // 3, tap % 3
            at = (2 - a) * wide + b * ch
            kern_t[:, at : at + ch] = kern[t, tap].T

    def back_row(t, r):
        base = pl.multiple_of(r * wide, wide)
        total = jnp.dot(kern_t[...], gs[pl.ds(base, 3 * wide), :], preferred_element_type=F32)
        value = jnp.where(sv[t, r].astype(F32) > 0, total, 0.0).astype(BF16)
        states[t, r] = value
        if t + 1 < TICKS:
            cur[t + 1, r] = jnp.where(restart[t + 1], fresh[t, r], value)

    def back_edges(t):
        def outer(i, carry):
            back_row(t, i * (height - 1))
            return carry

        lax.fori_loop(0, 2, outer, 0)
        if t + 1 < TICKS:
            halo_start(t + 1)

    def back_rest(t):
        def inner(i, carry):
            back_row(t, i + 1)
            return carry

        lax.fori_loop(0, height - 2, inner, 0)
        pltpu.make_async_copy(states.at[t], states_hbm.at[t, 0], st_sem.at[t]).start()

    def back(t):
        back_edges(t)
        back_rest(t)

    slab = ch // peers

    slot = (((0, 0), (0, 1)), ((0, 1), (1, 0)), ((1, 0), (1, 1)))

    def pick(even, odd):
        return even if even == odd else even + core * (odd - even)

    def along(values, t, a, k):
        even, odd = halving(bits, t, 0, a)[k], halving(bits, t, 1, a)[k]
        return values[even] if even == odd else values[even] + core * (values[odd] - values[even])

    def weight_rows(t, a):
        left = jnp.concatenate(
            [gs[(r + 2 - a) * wide : (r + 3 - a) * wide, :] for r in range(height)], axis=1
        )
        total = lax.dot_general(left, xs[...], (((1,), (1,)), ((), ())), preferred_element_type=F32)
        total = total * scale
        for b in range(3):
            for j in range(peers):
                at = b * ch + j * slab
                value = total[at : at + slab, :]
                at = pick(place(bits, *slot[t][0], a, j), place(bits, *slot[t][1], a, j))
                if t == TICKS - 1:
                    extra = sib[a, at, b].astype(F32)
                    value = value + jnp.where(core == 0, extra, 0.0)
                dk[t, a, at, b] = value.astype(BF16)

    def add_sibling(a):
        def step(j, carry):
            dk[0, a, j] = (dk[0, a, j].astype(F32) + sib[a, j].astype(F32)).astype(BF16)
            return carry

        lax.fori_loop(0, peers, step, 0)

    def rs_copy(t, a, k):
        count = peers >> (k + 1)
        source = dk.at[2 * t, a] if k == 0 else part.at[t, a, pl.ds(peers - (peers >> (k - 1)), peers >> k)]
        return pltpu.make_async_remote_copy(
            src_ref=source.at[pl.ds((1 - along(bit, t, a, k)) * count, count)],
            dst_ref=rx.at[t, a, pl.ds(peers - (peers >> k), count)],
            send_sem=rs_send.at[t, a, k],
            recv_sem=rs_recv.at[t, a, k],
            device_id={"rows": along(mate, t, a, k)},
            device_id_type=MESH,
        )

    def summed(t, a, k):
        count = peers >> (k + 1)
        rs_copy(t, a, k).wait_recv()
        at = along(bit, t, a, k) * count
        if k == 0:
            own = dk[2 * t, a, pl.ds(at, count)]
        else:
            own = part[t, a, pl.ds(at + peers - (peers >> (k - 1)), count)]
        return own.astype(F32) + rx[t, a, pl.ds(peers - (peers >> k), count)].astype(F32)

    def rs_step(t, a, k):
        count = peers >> (k + 1)
        part[t, a, pl.ds(peers - (peers >> k), count)] = summed(t, a, k).astype(BF16)
        rs_copy(t, a, k + 1).start()

    def rs_last(t, a):
        total = summed(t, a, bits - 1)[0]
        before = held[0, 3 * a : 3 * a + 3] if t == 0 else held_rx[3 * a : 3 * a + 3]
        value = (before.astype(F32) + total).astype(BF16)
        if t == 0:
            held[1, 3 * a : 3 * a + 3] = value
        else:
            out_ref[0, 3 * a : 3 * a + 3] = value

    order = (1, 0, 2)

    first = core == 0
    second = core == 1

    loads[0].wait()
    halo_start(0)
    loads[2].wait()
    kern_copy(0).start()
    turn_kernel(0)
    loads[1].wait()
    inner_rows(0)
    weight_rows(0, 1)
    loads[3].wait()

    @pl.when(first)
    def _():
        rs_copy(0, 1, 0).start()
        kern_copy(0).wait_recv()
        kern_copy(1).start()

    outer_rows(0)
    back_edges(0)
    for a in (0, 2):
        weight_rows(0, a)

        @pl.when(first)
        def _():
            rs_copy(0, a, 0).start()

    back_rest(0)
    loads[4].wait()
    inner_rows(1)
    weight_rows(1, 1)
    sib_copy(1).start()

    @pl.when(first)
    def _():
        rs_step(0, 1, 0)

    outer_rows(1)

    @pl.when(first)
    def _():
        turn_kernel(1)
        back_edges(1)

    for a in (0, 2):
        weight_rows(1, a)
        sib_copy(a).start()

    sib_copy(1).wait_recv()

    @pl.when(first)
    def _():
        rs_step(0, 0, 0)
        rs_step(0, 2, 0)

    @pl.when(second)
    def _():
        add_sibling(1)
        rs_copy(0, 1, 0).start()
        kern_copy(0).wait_recv()
        kern_copy(1).start()
        turn_kernel(1)
        back_edges(1)

    for a in (0, 2):
        sib_copy(a).wait_recv()

        @pl.when(second)
        def _():
            add_sibling(a)
            rs_copy(0, a, 0).start()

    back_rest(1)
    loads[5].wait()
    loads[6].wait()
    inner_rows(2)
    weight_rows(2, 1)
    rs_copy(1, 1, 0).start()

    @pl.when(first)
    def _():
        for k in range(1, bits - 1):
            rs_step(0, 1, k)

    @pl.when(second)
    def _():
        rs_step(0, 1, 0)

    outer_rows(2)
    for a in (0, 2):
        weight_rows(2, a)
        rs_copy(1, a, 0).start()

    @pl.when(first)
    def _():
        for k in range(1, bits - 1):
            rs_step(0, 0, k)
            rs_step(0, 2, k)
        kern_copy(1).wait_recv()
        turn_kernel(2)
        back(2)
        rs_step(1, 1, 0)

    @pl.when(second)
    def _():
        for k in range(1, bits - 1):
            rs_step(0, 1, k)
        rs_step(0, 0, 0)
        rs_step(0, 2, 0)
        rs_step(1, 1, 0)
        for k in range(1, bits - 1):
            rs_step(0, 0, k)
            rs_step(0, 2, k)

    for a in (0, 2):
        rs_step(1, a, 0)
    for k in range(1, bits - 1):
        rs_step(1, 1, k)
    for a in order:
        rs_last(0, a)
    held_copy.start()

    @pl.when(second)
    def _():
        kern_copy(1).wait_recv()
        turn_kernel(2)
        back(2)

    for k in range(1, bits - 1):
        for a in (0, 2):
            rs_step(1, a, k)

    held_copy.wait_recv()
    for a in order:
        rs_last(1, a)

    for t in range(TICKS):
        pltpu.make_async_copy(states.at[t], states_hbm.at[t, 0], st_sem.at[t]).wait()
        @pl.when(has_up)
        def _():
            halo_copy(t, 1).wait_send()

        @pl.when(has_down)
        def _():
            halo_copy(t, 0).wait_send()

    for t in range(TICKS - 1):
        kern_copy(t).wait_send()
        for a in range(3):
            for k in range(bits):
                rs_copy(t, a, k).wait_send()
    for a in range(3):
        sib_copy(a).wait_send()
    held_copy.wait_send()


def shards(section_weights, grad_acc, saved_inputs, cotangent, fresh_grads):
    peers = lax.axis_size("rows")
    cycle = lax.axis_size("blk")
    ticks, _, height, ch, cols = saved_inputs.shape
    bits = peers.bit_length() - 1
    slab = ch // peers
    scale = float(peers * height * cols) ** (-0.5)
    weights = section_weights.transpose(0, 2, 1, 3)
    held = grad_acc.transpose(0, 2, 1, 3)
    anywhere = pl.BlockSpec(memory_space=pl.ANY)
    dma = pltpu.SemaphoreType.DMA
    states, out = pl.pallas_call(
        functools.partial(kernel, (peers, cycle, height, ch, cols, scale)),
        out_shape=(
            jax.ShapeDtypeStruct(saved_inputs.shape, BF16),
            jax.ShapeDtypeStruct(held.shape, BF16),
        ),
        in_specs=[anywhere] * 5,
        out_specs=(anywhere, pl.BlockSpec(memory_space=pltpu.VMEM)),
        scratch_shapes=[
            pltpu.VMEM((ticks, 9, ch, ch), BF16),
            pltpu.VMEM((ch, 9 * ch), BF16),
            pltpu.VMEM((ticks, height, ch, cols), BF16),
            pltpu.VMEM((ticks, height, ch, cols), BF16),
            pltpu.VMEM((ticks - 1, height, ch, cols), BF16),
            pltpu.VMEM((ch, height * cols), BF16),
            pltpu.VMEM(((height + 2) * 3 * ch, cols), BF16),
            pltpu.VMEM((ticks, 2, ch, cols), BF16),
            pltpu.VMEM((ticks, height, ch, cols), BF16),
            pltpu.VMEM((ticks, 3, peers, 3, slab, ch), BF16),
            pltpu.VMEM((2, 3, peers, 3, slab, ch), BF16),
            pltpu.VMEM((2, 3, peers, 3, slab, ch), BF16),
            pltpu.VMEM((3, peers, 3, slab, ch), BF16),
            pltpu.VMEM((2, 9, slab, ch), BF16),
            pltpu.VMEM((9, slab, ch), BF16),
            dma((7,)),
            dma((ticks, 2)),
            dma((ticks, 2)),
            dma((ticks - 1,)),
            dma((ticks - 1,)),
            dma((2, 3, bits)),
            dma((2, 3, bits)),
            dma,
            dma,
            dma((3,)),
            dma((3,)),
            dma((ticks,)),
        ],
        compiler_params=pltpu.CompilerParams(collective_id=0, has_side_effects=True),
    )(weights, held, saved_inputs, cotangent, fresh_grads)
    return states, out.transpose(0, 2, 1, 3)


def solution(mesh):
    return jax.shard_map(
        shards,
        mesh=mesh,
        in_specs=(
            P("blk", None, None, None),
            P("blk", "rows", None, None),
            P(None, "blk", "rows", None, None),
            P("blk", "rows", None, None),
            P(None, "rows", None, None),
        ),
        out_specs=(P(None, "blk", "rows", None, None), P("blk", "rows", None, None)),
        check_vma=False,
    )
```

```python
import functools

import jax
import jax.numpy as jnp
from jax import lax
from jax.experimental import pallas as pl
from jax.experimental.pallas import tpu as pltpu
from jax.sharding import PartitionSpec as P

TICKS = 3
MESH = pl.DeviceIdType.MESH
F32 = jnp.float32
BF16 = jnp.bfloat16


LATE = {(0, 0): (0, 1, 2), (0, 1): (0, 1, 2), (1, 0): (2,), (1, 1): (2,)}
EARLY = (1, 0)
TURN = (2, 0)


def halving(bits, t, core, a):
    return [*range(1, bits), 0] if a in LATE[t, core] else list(range(bits))


def place(bits, t, core, a, value):
    return sum(((value >> k) & 1) << (bits - 1 - at) for at, k in enumerate(halving(bits, t, core, a)))


def kernel(
    shape, w_hbm, acc_hbm, saved_hbm, cot_hbm, fresh_hbm, states, out_ref,
    kern, kern_t, sv, cur, fresh, xs, gs, halo, dk, rx, part, sib, held, held_rx, early,
    load_sem, halo_send, halo_recv, k_send, k_recv, rs_send, rs_recv, acc_send, acc_recv, sib_send, sib_recv, early_send, early_recv,
):
    peers, cycle, height, ch, cols, scale = shape
    bits = peers.bit_length() - 1
    row = lax.axis_index("rows")
    pos = lax.axis_index("blk")
    below = lax.rem(pos + cycle - 1, cycle)
    bit = [lax.rem(row // (1 << k), 2) for k in range(bits)]
    mate = [row + (1 - 2 * bit[k]) * (1 << k) for k in range(bits)]
    has_up = row > 0
    has_down = row < peers - 1
    restart = [None] + [pos == (cycle - t) % cycle for t in range(1, TICKS)]

    loads = [
        pltpu.make_async_copy(cot_hbm.at[0], cur.at[0], load_sem.at[0]),
        pltpu.make_async_copy(saved_hbm.at[0, 0], sv.at[0], load_sem.at[1]),
        pltpu.make_async_copy(w_hbm.at[0], kern.at[0], load_sem.at[2]),
        pltpu.make_async_copy(fresh_hbm, fresh, load_sem.at[3]),
        pltpu.make_async_copy(saved_hbm.at[1, 0], sv.at[1], load_sem.at[4]),
        pltpu.make_async_copy(saved_hbm.at[2, 0], sv.at[2], load_sem.at[5]),
        pltpu.make_async_copy(acc_hbm.at[0], held.at[0], load_sem.at[6]),
    ]
    for load in loads:
        load.start()

    barrier = pltpu.get_barrier_semaphore()
    core = lax.rem(pos, 2)
    sibling = pos + 1 - 2 * core
    far = lax.rem(pos + cycle - (TICKS - 1), cycle)
    hops = sorted({d % cycle for d in (1, -1, TICKS - 1, 1 - TICKS)})
    greet = [{"blk": lax.rem(pos + d, cycle)} for d in hops] + [{"rows": m} for m in mate]
    for who in greet:
        pl.semaphore_signal(barrier, inc=1, device_id=who, device_id_type=MESH)

    other = row + 2 * bit[0] - 1
    has_other = jnp.logical_and(other >= 0, other < peers)

    @pl.when(has_other)
    def _():
        pl.semaphore_signal(barrier, inc=1, device_id={"rows": other}, device_id_type=MESH)

    pl.semaphore_wait(barrier, len(greet) + has_other.astype(jnp.int32))

    def halo_copy(t, side):
        edge = 0 if side == 1 else height - 1
        return pltpu.make_async_remote_copy(
            src_ref=cur.at[t, edge],
            dst_ref=halo.at[t, side],
            send_sem=halo_send.at[t, side],
            recv_sem=halo_recv.at[t, side],
            device_id={"rows": row - 1 if side == 1 else row + 1},
            device_id_type=MESH,
        )

    def halo_start(t):
        @pl.when(has_up)
        def _():
            halo_copy(t, 1).start()

        @pl.when(has_down)
        def _():
            halo_copy(t, 0).start()

    def kern_copy(t):
        return pltpu.make_async_remote_copy(
            src_ref=kern.at[t],
            dst_ref=kern.at[t + 1],
            send_sem=k_send.at[t],
            recv_sem=k_recv.at[t],
            device_id={"blk": below},
            device_id_type=MESH,
        )

    held_copy = pltpu.make_async_remote_copy(
        src_ref=held.at[1],
        dst_ref=held_rx,
        send_sem=acc_send,
        recv_sem=acc_recv,
        device_id={"blk": far},
        device_id_type=MESH,
    )

    def sib_copy(a):
        return pltpu.make_async_remote_copy(
            src_ref=dk.at[1, a],
            dst_ref=sib.at[a],
            send_sem=sib_send.at[a],
            recv_sem=sib_recv.at[a],
            device_id={"blk": sibling},
            device_id_type=MESH,
        )

    def early_copy(a):
        return pltpu.make_async_remote_copy(
            src_ref=dk.at[0, a],
            dst_ref=early.at[a],
            send_sem=early_send.at[a],
            recv_sem=early_recv.at[a],
            device_id={"blk": far},
            device_id_type=MESH,
        )

    wide = 3 * ch
    lane = lax.broadcasted_iota(jnp.int32, (ch, cols), 1)

    def put_row(index, value):
        base = pl.multiple_of(index * wide, wide)
        full = value.astype(F32)
        left = jnp.where(lane == cols - 1, 0.0, pltpu.roll(full, cols - 1, 1))
        right = jnp.where(lane == 0, 0.0, pltpu.roll(full, 1, 1))
        gs[pl.ds(base, ch), :] = left.astype(BF16)
        gs[pl.ds(base + ch, ch), :] = value
        gs[pl.ds(base + 2 * ch, ch), :] = right.astype(BF16)

    def inner_rows(t):
        def step(r, carry):
            put_row(r + 1, cur[t, r])
            return carry

        lax.fori_loop(0, height, step, 0)
        for r in range(height):
            xs[:, r * cols : (r + 1) * cols] = jnp.maximum(sv[t, r], 0)

    def outer_rows(t):
        for side, have, index in ((0, has_up, 0), (1, has_down, height + 1)):
            @pl.when(have)
            def _():
                halo_copy(t, side).wait_recv()
                put_row(index, halo[t, side])

            @pl.when(jnp.logical_not(have))
            def _():
                gs[index * wide : (index + 1) * wide, :] = jnp.zeros((wide, cols), BF16)

    def turn_kernel(t):
        for tap in range(9):
            a, b = tap // 3, tap % 3
            at = (2 - a) * wide + b * ch
            kern_t[:, at : at + ch] = kern[t, tap].T

    def back_row(t, r):
        base = pl.multiple_of(r * wide, wide)
        total = jnp.dot(kern_t[...], gs[pl.ds(base, 3 * wide), :], preferred_element_type=F32)
        value = jnp.where(sv[t, r].astype(F32) > 0, total, 0.0).astype(BF16)
        states[t, 0, r] = value
        if t + 1 < TICKS:
            cur[t + 1, r] = jnp.where(restart[t + 1], fresh[t, r], value)

    def back_edges(t):
        def outer(i, carry):
            back_row(t, i * (height - 1))
            return carry

        lax.fori_loop(0, 2, outer, 0)
        if t + 1 < TICKS:
            halo_start(t + 1)

    def back_rest(t):
        def inner(i, carry):
            back_row(t, i + 1)
            return carry

        lax.fori_loop(0, height - 2, inner, 0)

    def back(t):
        back_edges(t)
        back_rest(t)

    slab = ch // peers

    odd_slot = ((0, 1), (1, 0), (1, 1))

    def even_slot(t, a):
        return ((1, 0) if a in EARLY else (0, 0), (0, 1), (1, 0))[t]

    def pick(even, odd):
        return even if even == odd else even + core * (odd - even)

    def along(values, t, a, k):
        even, odd = halving(bits, t, 0, a)[k], halving(bits, t, 1, a)[k]
        return values[even] if even == odd else values[even] + core * (values[odd] - values[even])

    def weight_rows(t, a):
        left = jnp.concatenate(
            [gs[(r + 2 - a) * wide : (r + 3 - a) * wide, :] for r in range(height)], axis=1
        )
        total = lax.dot_general(left, xs[...], (((1,), (1,)), ((), ())), preferred_element_type=F32)
        total = total * scale
        for b in range(3):
            for j in range(peers):
                at = b * ch + j * slab
                value = total[at : at + slab, :]
                at = pick(place(bits, *even_slot(t, a), a, j), place(bits, *odd_slot[t], a, j))
                if t == TICKS - 1:
                    extra = sib[a, at, b].astype(F32)
                    if a in EARLY:
                        extra = extra + early[a, at, b].astype(F32)
                    value = value + jnp.where(core == 0, extra, 0.0)
                dk[t, a, at, b] = value.astype(BF16)

    def add_sibling(a):
        def step(j, carry):
            dk[0, a, j] = (dk[0, a, j].astype(F32) + sib[a, j].astype(F32)).astype(BF16)
            return carry

        lax.fori_loop(0, peers, step, 0)

    def rs_copy(t, a, k):
        count = peers >> (k + 1)
        source = dk.at[2 * t, a] if k == 0 else part.at[t, a, pl.ds(peers - (peers >> (k - 1)), peers >> k)]
        return pltpu.make_async_remote_copy(
            src_ref=source.at[pl.ds((1 - along(bit, t, a, k)) * count, count)],
            dst_ref=rx.at[t, a, pl.ds(peers - (peers >> k), count)],
            send_sem=rs_send.at[t, a, k],
            recv_sem=rs_recv.at[t, a, k],
            device_id={"rows": along(mate, t, a, k)},
            device_id_type=MESH,
        )

    def summed(t, a, k):
        count = peers >> (k + 1)
        rs_copy(t, a, k).wait_recv()
        at = along(bit, t, a, k) * count
        if k == 0:
            own = dk[2 * t, a, pl.ds(at, count)]
        else:
            own = part[t, a, pl.ds(at + peers - (peers >> (k - 1)), count)]
        return own.astype(F32) + rx[t, a, pl.ds(peers - (peers >> k), count)].astype(F32)

    def rs_step(t, a, k):
        count = peers >> (k + 1)
        part[t, a, pl.ds(peers - (peers >> k), count)] = summed(t, a, k).astype(BF16)
        rs_copy(t, a, k + 1).start()

    def rs_last(t, a):
        total = summed(t, a, bits - 1)[0]
        before = held[0, 3 * a : 3 * a + 3] if t == 0 else held_rx[3 * a : 3 * a + 3]
        value = (before.astype(F32) + total).astype(BF16)
        if t == 0:
            held[1, 3 * a : 3 * a + 3] = value
        else:
            out_ref[0, 3 * a : 3 * a + 3] = value

    order = (1, 0, 2)

    first = core == 0
    second = core == 1

    def launch(a):
        @pl.when(first)
        def _():
            if a in EARLY:
                early_copy(a).start()
            else:
                rs_copy(0, a, 0).start()

    rest = [a for a in order if a not in EARLY]

    loads[0].wait()
    halo_start(0)
    loads[2].wait()
    kern_copy(0).start()
    turn_kernel(0)
    loads[1].wait()
    inner_rows(0)
    weight_rows(0, 1)
    launch(1)
    loads[3].wait()
    outer_rows(0)
    back_edges(0)
    for a in (0, 2):
        weight_rows(0, a)
        launch(a)

    @pl.when(first)
    def _():
        kern_copy(0).wait_recv()
        kern_copy(1).start()

    back_rest(0)
    loads[4].wait()
    inner_rows(1)
    weight_rows(1, 1)
    sib_copy(1).start()
    outer_rows(1)

    @pl.when(first)
    def _():
        turn_kernel(1)
        back_edges(1)

    for a in (0, 2):
        weight_rows(1, a)
        sib_copy(a).start()

    sib_copy(1).wait_recv()

    @pl.when(first)
    def _():
        for a in rest:
            rs_step(0, a, 0)

    @pl.when(second)
    def _():
        add_sibling(1)
        rs_copy(0, 1, 0).start()
        kern_copy(0).wait_recv()
        kern_copy(1).start()
        turn_kernel(1)
        back_edges(1)

    for a in (0, 2):
        sib_copy(a).wait_recv()

        @pl.when(second)
        def _():
            add_sibling(a)
            rs_copy(0, a, 0).start()

    back_rest(1)
    loads[5].wait()
    loads[6].wait()
    inner_rows(2)

    def last_rows(a):
        if a in EARLY:
            @pl.when(first)
            def _():
                early_copy(a).wait_recv()

        weight_rows(2, a)
        rs_copy(1, a, 0).start()

    last_rows(1)

    @pl.when(first)
    def _():
        for k in range(1, bits - 1):
            for a in rest:
                rs_step(0, a, k)

    @pl.when(second)
    def _():
        rs_step(0, 1, 0)

    outer_rows(2)
    @pl.when(first)
    def _():
        kern_copy(1).wait_recv()
        turn_kernel(2)

    for a in (0, 2):
        last_rows(a)

    @pl.when(first)
    def _():
        back(2)
        rs_step(1, 1, 0)

    @pl.when(second)
    def _():
        for k in range(1, bits - 1):
            rs_step(0, 1, k)
        rs_step(0, 0, 0)
        rs_step(0, 2, 0)
        rs_step(1, 1, 0)
        for k in range(1, bits - 1):
            rs_step(0, 0, k)
            rs_step(0, 2, k)

    for a in TURN:
        rs_step(1, a, 0)
    for k in range(1, bits - 1):
        rs_step(1, 1, k)

    @pl.when(first)
    def _():
        for a in EARLY:
            held[1, 3 * a : 3 * a + 3] = held[0, 3 * a : 3 * a + 3]
        for a in rest:
            rs_last(0, a)

    @pl.when(second)
    def _():
        for a in order:
            rs_last(0, a)

    held_copy.start()

    for k in range(1, bits - 1):
        for a in TURN:
            rs_step(1, a, k)

    @pl.when(second)
    def _():
        kern_copy(1).wait_recv()
        turn_kernel(2)
        back(2)

    held_copy.wait_recv()
    for a in (1, *TURN):
        rs_last(1, a)

    for t in range(TICKS):
        @pl.when(has_up)
        def _():
            halo_copy(t, 1).wait_send()

        @pl.when(has_down)
        def _():
            halo_copy(t, 0).wait_send()

    for t in range(TICKS - 1):
        kern_copy(t).wait_send()
    for a in range(3):
        sib_copy(a).wait_send()
        for k in range(bits):
            rs_copy(1, a, k).wait_send()
    held_copy.wait_send()

    @pl.when(first)
    def _():
        for a in range(3):
            if a in EARLY:
                early_copy(a).wait_send()
            else:
                for k in range(bits):
                    rs_copy(0, a, k).wait_send()

    @pl.when(second)
    def _():
        for a in range(3):
            for k in range(bits):
                rs_copy(0, a, k).wait_send()


def shards(section_weights, grad_acc, saved_inputs, cotangent, fresh_grads):
    peers = lax.axis_size("rows")
    cycle = lax.axis_size("blk")
    ticks, _, height, ch, cols = saved_inputs.shape
    bits = peers.bit_length() - 1
    slab = ch // peers
    scale = float(peers * height * cols) ** (-0.5)
    weights = section_weights.transpose(0, 2, 1, 3)
    held = grad_acc.transpose(0, 2, 1, 3)
    anywhere = pl.BlockSpec(memory_space=pl.ANY)
    dma = pltpu.SemaphoreType.DMA
    states, out = pl.pallas_call(
        functools.partial(kernel, (peers, cycle, height, ch, cols, scale)),
        out_shape=(
            pltpu.VMEM(saved_inputs.shape, BF16),
            pltpu.VMEM(held.shape, BF16),
        ),
        in_specs=[anywhere] * 5,
        out_specs=(pl.BlockSpec(memory_space=pltpu.VMEM), pl.BlockSpec(memory_space=pltpu.VMEM)),
        scratch_shapes=[
            pltpu.VMEM((ticks, 9, ch, ch), BF16),
            pltpu.VMEM((ch, 9 * ch), BF16),
            pltpu.VMEM((ticks, height, ch, cols), BF16),
            pltpu.VMEM((ticks, height, ch, cols), BF16),
            pltpu.VMEM((ticks - 1, height, ch, cols), BF16),
            pltpu.VMEM((ch, height * cols), BF16),
            pltpu.VMEM(((height + 2) * 3 * ch, cols), BF16),
            pltpu.VMEM((ticks, 2, ch, cols), BF16),
            pltpu.VMEM((ticks, 3, peers, 3, slab, ch), BF16),
            pltpu.VMEM((2, 3, peers, 3, slab, ch), BF16),
            pltpu.VMEM((2, 3, peers, 3, slab, ch), BF16),
            pltpu.VMEM((3, peers, 3, slab, ch), BF16),
            pltpu.VMEM((2, 9, slab, ch), BF16),
            pltpu.VMEM((9, slab, ch), BF16),
            pltpu.VMEM((3, peers, 3, slab, ch), BF16),
            dma((7,)),
            dma((ticks, 2)),
            dma((ticks, 2)),
            dma((ticks - 1,)),
            dma((ticks - 1,)),
            dma((2, 3, bits)),
            dma((2, 3, bits)),
            dma,
            dma,
            dma((3,)),
            dma((3,)),
            dma((3,)),
            dma((3,)),
        ],
        compiler_params=pltpu.CompilerParams(collective_id=0, has_side_effects=True),
    )(weights, held, saved_inputs, cotangent, fresh_grads)
    return states, out.transpose(0, 2, 1, 3)


def solution(mesh):
    return jax.shard_map(
        shards,
        mesh=mesh,
        in_specs=(
            P("blk", None, None, None),
            P("blk", "rows", None, None),
            P(None, "blk", "rows", None, None),
            P("blk", "rows", None, None),
            P(None, "rows", None, None),
        ),
        out_specs=(P(None, "blk", "rows", None, None), P("blk", "rows", None, None)),
        check_vma=False,
    )
```

```python
import functools

import jax
import jax.numpy as jnp
from jax import lax
from jax.experimental import pallas as pl
from jax.experimental.pallas import tpu as pltpu
from jax.sharding import PartitionSpec as P

TICKS = 3
MESH = pl.DeviceIdType.MESH
F32 = jnp.float32
BF16 = jnp.bfloat16


LATE = {(0, 0): (0, 1, 2), (0, 1): (0, 1, 2), (1, 0): (2,), (1, 1): (2,)}
EARLY = (1, 0)
TURN = (2, 0)


def halving(bits, t, core, a):
    return [*range(1, bits), 0] if a in LATE[t, core] else list(range(bits))


def place(bits, t, core, a, value):
    return sum(((value >> k) & 1) << (bits - 1 - at) for at, k in enumerate(halving(bits, t, core, a)))


def kernel(
    shape, w_hbm, acc_hbm, saved_hbm, cot_hbm, fresh_hbm, states, out_ref,
    kern, kern_t, sv, cur, fresh, xs, gs, halo, dk, rx, part, sib, held, held_rx, early,
    load_sem, halo_send, halo_recv, k_send, k_recv, rs_send, rs_recv, acc_send, acc_recv, sib_send, sib_recv, early_send, early_recv,
):
    peers, cycle, height, ch, cols, scale = shape
    bits = peers.bit_length() - 1
    row = lax.axis_index("rows")
    pos = lax.axis_index("blk")
    below = lax.rem(pos + cycle - 1, cycle)
    bit = [lax.rem(row // (1 << k), 2) for k in range(bits)]
    mate = [row + (1 - 2 * bit[k]) * (1 << k) for k in range(bits)]
    has_up = row > 0
    has_down = row < peers - 1
    restart = [None] + [pos == (cycle - t) % cycle for t in range(1, TICKS)]

    loads = [
        pltpu.make_async_copy(cot_hbm.at[0], cur.at[0], load_sem.at[0]),
        pltpu.make_async_copy(saved_hbm.at[0, 0], sv.at[0], load_sem.at[1]),
        pltpu.make_async_copy(w_hbm.at[0], kern.at[0], load_sem.at[2]),
        pltpu.make_async_copy(fresh_hbm, fresh, load_sem.at[3]),
        pltpu.make_async_copy(saved_hbm.at[1, 0], sv.at[1], load_sem.at[4]),
        pltpu.make_async_copy(saved_hbm.at[2, 0], sv.at[2], load_sem.at[5]),
        pltpu.make_async_copy(acc_hbm.at[0], held.at[0], load_sem.at[6]),
    ]
    for load in loads:
        load.start()

    barrier = pltpu.get_barrier_semaphore()
    core = lax.rem(pos, 2)
    sibling = pos + 1 - 2 * core
    far = lax.rem(pos + cycle - (TICKS - 1), cycle)
    hops = sorted({d % cycle for d in (1, -1, TICKS - 1, 1 - TICKS)})
    greet = [{"blk": lax.rem(pos + d, cycle)} for d in hops] + [{"rows": m} for m in mate]
    for who in greet:
        pl.semaphore_signal(barrier, inc=1, device_id=who, device_id_type=MESH)

    other = row + 2 * bit[0] - 1
    has_other = jnp.logical_and(other >= 0, other < peers)

    @pl.when(has_other)
    def _():
        pl.semaphore_signal(barrier, inc=1, device_id={"rows": other}, device_id_type=MESH)

    pl.semaphore_wait(barrier, len(greet) + has_other.astype(jnp.int32))

    def halo_copy(t, side):
        edge = 0 if side == 1 else height - 1
        return pltpu.make_async_remote_copy(
            src_ref=cur.at[t, edge],
            dst_ref=halo.at[t, side],
            send_sem=halo_send.at[t, side],
            recv_sem=halo_recv.at[t, side],
            device_id={"rows": row - 1 if side == 1 else row + 1},
            device_id_type=MESH,
        )

    def halo_start(t):
        @pl.when(has_up)
        def _():
            halo_copy(t, 1).start()

        @pl.when(has_down)
        def _():
            halo_copy(t, 0).start()

    def kern_copy(t):
        return pltpu.make_async_remote_copy(
            src_ref=kern.at[t],
            dst_ref=kern.at[t + 1],
            send_sem=k_send.at[t],
            recv_sem=k_recv.at[t],
            device_id={"blk": below},
            device_id_type=MESH,
        )

    held_copy = pltpu.make_async_remote_copy(
        src_ref=held.at[1],
        dst_ref=held_rx,
        send_sem=acc_send,
        recv_sem=acc_recv,
        device_id={"blk": far},
        device_id_type=MESH,
    )

    def sib_copy(a):
        return pltpu.make_async_remote_copy(
            src_ref=dk.at[1, a],
            dst_ref=sib.at[a],
            send_sem=sib_send.at[a],
            recv_sem=sib_recv.at[a],
            device_id={"blk": sibling},
            device_id_type=MESH,
        )

    def early_copy(a):
        return pltpu.make_async_remote_copy(
            src_ref=dk.at[0, a],
            dst_ref=early.at[a],
            send_sem=early_send.at[a],
            recv_sem=early_recv.at[a],
            device_id={"blk": far},
            device_id_type=MESH,
        )

    wide = 3 * ch
    lane = lax.broadcasted_iota(jnp.int32, (ch, cols), 1)

    def put_row(index, value):
        base = pl.multiple_of(index * wide, wide)
        full = value.astype(F32)
        left = jnp.where(lane == cols - 1, 0.0, pltpu.roll(full, cols - 1, 1))
        right = jnp.where(lane == 0, 0.0, pltpu.roll(full, 1, 1))
        gs[pl.ds(base, ch), :] = left.astype(BF16)
        gs[pl.ds(base + ch, ch), :] = value
        gs[pl.ds(base + 2 * ch, ch), :] = right.astype(BF16)

    def inner_rows(t):
        def step(r, carry):
            put_row(r + 1, cur[t, r])
            return carry

        lax.fori_loop(0, height, step, 0)
        for r in range(height):
            xs[:, r * cols : (r + 1) * cols] = jnp.maximum(sv[t, r], 0)

    def outer_rows(t):
        for side, have, index in ((0, has_up, 0), (1, has_down, height + 1)):
            @pl.when(have)
            def _():
                halo_copy(t, side).wait_recv()
                put_row(index, halo[t, side])

            @pl.when(jnp.logical_not(have))
            def _():
                gs[index * wide : (index + 1) * wide, :] = jnp.zeros((wide, cols), BF16)

    def turn_kernel(t):
        for tap in range(9):
            a, b = tap // 3, tap % 3
            at = (2 - a) * wide + b * ch
            kern_t[:, at : at + ch] = kern[t, tap].T

    def back_row(t, r):
        base = pl.multiple_of(r * wide, wide)
        total = jnp.dot(kern_t[...], gs[pl.ds(base, 3 * wide), :], preferred_element_type=F32)
        value = jnp.where(sv[t, r].astype(F32) > 0, total, 0.0).astype(BF16)
        states[t, 0, r] = value
        if t + 1 < TICKS:
            cur[t + 1, r] = jnp.where(restart[t + 1], fresh[t, r], value)

    def back_edges(t):
        def outer(i, carry):
            back_row(t, i * (height - 1))
            return carry

        lax.fori_loop(0, 2, outer, 0)
        if t + 1 < TICKS:
            halo_start(t + 1)

    def back_rest(t):
        def inner(i, carry):
            back_row(t, i + 1)
            return carry

        lax.fori_loop(0, height - 2, inner, 0)

    def back(t):
        back_edges(t)
        back_rest(t)

    slab = ch // peers

    odd_slot = ((0, 1), (1, 0), (1, 1))

    def even_slot(t, a):
        return ((1, 0) if a in EARLY else (0, 0), (0, 1), (1, 0))[t]

    def pick(even, odd):
        return even if even == odd else even + core * (odd - even)

    def along(values, t, a, k):
        even, odd = halving(bits, t, 0, a)[k], halving(bits, t, 1, a)[k]
        return values[even] if even == odd else values[even] + core * (values[odd] - values[even])

    def weight_rows(t, a):
        left = jnp.concatenate(
            [gs[(r + 2 - a) * wide : (r + 3 - a) * wide, :] for r in range(height)], axis=1
        )
        total = lax.dot_general(left, xs[...], (((1,), (1,)), ((), ())), preferred_element_type=F32)
        total = total * scale
        for b in range(3):
            for j in range(peers):
                at = b * ch + j * slab
                value = total[at : at + slab, :]
                at = pick(place(bits, *even_slot(t, a), a, j), place(bits, *odd_slot[t], a, j))
                if t == TICKS - 1:
                    extra = sib[a, at, b].astype(F32)
                    if a in EARLY:
                        extra = extra + early[a, at, b].astype(F32)
                    value = value + jnp.where(core == 0, extra, 0.0)
                dk[t, a, at, b] = value.astype(BF16)

    def add_sibling(a):
        def step(j, carry):
            dk[0, a, j] = (dk[0, a, j].astype(F32) + sib[a, j].astype(F32)).astype(BF16)
            return carry

        lax.fori_loop(0, peers, step, 0)

    def rs_copy(t, a, k):
        count = peers >> (k + 1)
        source = dk.at[2 * t, a] if k == 0 else part.at[t, a, pl.ds(peers - (peers >> (k - 1)), peers >> k)]
        return pltpu.make_async_remote_copy(
            src_ref=source.at[pl.ds((1 - along(bit, t, a, k)) * count, count)],
            dst_ref=rx.at[t, a, pl.ds(peers - (peers >> k), count)],
            send_sem=rs_send.at[t, a, k],
            recv_sem=rs_recv.at[t, a, k],
            device_id={"rows": along(mate, t, a, k)},
            device_id_type=MESH,
        )

    def summed(t, a, k):
        count = peers >> (k + 1)
        rs_copy(t, a, k).wait_recv()
        at = along(bit, t, a, k) * count
        if k == 0:
            own = dk[2 * t, a, pl.ds(at, count)]
        else:
            own = part[t, a, pl.ds(at + peers - (peers >> (k - 1)), count)]
        return own.astype(F32) + rx[t, a, pl.ds(peers - (peers >> k), count)].astype(F32)

    def rs_step(t, a, k):
        count = peers >> (k + 1)
        part[t, a, pl.ds(peers - (peers >> k), count)] = summed(t, a, k).astype(BF16)
        rs_copy(t, a, k + 1).start()

    def rs_last(t, a):
        total = summed(t, a, bits - 1)[0]
        before = held[0, 3 * a : 3 * a + 3] if t == 0 else held_rx[3 * a : 3 * a + 3]
        value = (before.astype(F32) + total).astype(BF16)
        if t == 0:
            held[1, 3 * a : 3 * a + 3] = value
        else:
            out_ref[0, 3 * a : 3 * a + 3] = value

    order = (1, 0, 2)

    first = core == 0
    second = core == 1

    def launch(a):
        @pl.when(first)
        def _():
            if a in EARLY:
                early_copy(a).start()
            else:
                rs_copy(0, a, 0).start()

    rest = [a for a in order if a not in EARLY]

    loads[0].wait()
    halo_start(0)
    loads[2].wait()
    kern_copy(0).start()
    turn_kernel(0)
    loads[1].wait()
    inner_rows(0)
    weight_rows(0, 1)
    launch(1)
    loads[3].wait()
    outer_rows(0)
    back_edges(0)
    for a in (0, 2):
        weight_rows(0, a)
        launch(a)

    @pl.when(first)
    def _():
        kern_copy(0).wait_recv()
        kern_copy(1).start()

    back_rest(0)
    loads[4].wait()
    inner_rows(1)
    weight_rows(1, 1)
    sib_copy(1).start()
    outer_rows(1)

    @pl.when(first)
    def _():
        turn_kernel(1)
        back_edges(1)

    for a in (0, 2):
        weight_rows(1, a)
        sib_copy(a).start()

    sib_copy(1).wait_recv()

    @pl.when(first)
    def _():
        for a in rest:
            rs_step(0, a, 0)

    @pl.when(second)
    def _():
        add_sibling(1)
        rs_copy(0, 1, 0).start()
        kern_copy(0).wait_recv()
        kern_copy(1).start()
        turn_kernel(1)
        back_edges(1)

    for a in (0, 2):
        sib_copy(a).wait_recv()

        @pl.when(second)
        def _():
            add_sibling(a)
            rs_copy(0, a, 0).start()

    back_rest(1)
    loads[5].wait()
    loads[6].wait()
    inner_rows(2)

    def last_rows(a):
        if a in EARLY:
            @pl.when(first)
            def _():
                early_copy(a).wait_recv()

        weight_rows(2, a)
        rs_copy(1, a, 0).start()

    last_rows(1)

    @pl.when(first)
    def _():
        for k in range(1, bits - 1):
            for a in rest:
                rs_step(0, a, k)

    @pl.when(second)
    def _():
        rs_step(0, 1, 0)

    outer_rows(2)
    @pl.when(first)
    def _():
        kern_copy(1).wait_recv()
        turn_kernel(2)

    for a in (0, 2):
        last_rows(a)

    @pl.when(first)
    def _():
        back(2)
        rs_step(1, 1, 0)

    @pl.when(second)
    def _():
        for k in range(1, bits - 1):
            rs_step(0, 1, k)
        rs_step(0, 0, 0)
        rs_step(0, 2, 0)
        rs_step(1, 1, 0)
        for k in range(1, bits - 1):
            rs_step(0, 0, k)
            rs_step(0, 2, k)

    for a in TURN:
        rs_step(1, a, 0)
    for k in range(1, bits - 1):
        rs_step(1, 1, k)

    @pl.when(first)
    def _():
        for a in EARLY:
            held[1, 3 * a : 3 * a + 3] = held[0, 3 * a : 3 * a + 3]
        for a in rest:
            rs_last(0, a)

    @pl.when(second)
    def _():
        for a in order:
            rs_last(0, a)

    held_copy.start()

    for k in range(1, bits - 1):
        for a in TURN:
            rs_step(1, a, k)

    @pl.when(second)
    def _():
        kern_copy(1).wait_recv()
        turn_kernel(2)
        back(2)

    held_copy.wait_recv()
    for a in (1, *TURN):
        rs_last(1, a)

    for t in range(TICKS):
        @pl.when(has_up)
        def _():
            halo_copy(t, 1).wait_send()

        @pl.when(has_down)
        def _():
            halo_copy(t, 0).wait_send()

    for t in range(TICKS - 1):
        kern_copy(t).wait_send()
    for a in range(3):
        sib_copy(a).wait_send()
        for k in range(bits):
            rs_copy(1, a, k).wait_send()
    held_copy.wait_send()

    @pl.when(first)
    def _():
        for a in range(3):
            if a in EARLY:
                early_copy(a).wait_send()
            else:
                for k in range(bits):
                    rs_copy(0, a, k).wait_send()

    @pl.when(second)
    def _():
        for a in range(3):
            for k in range(bits):
                rs_copy(0, a, k).wait_send()


def store(states, out, states_hbm, out_hbm, sem):
    copies = [pltpu.make_async_copy(out, out_hbm, sem.at[0])]
    for t in range(TICKS):
        copies.append(pltpu.make_async_copy(states.at[t], states_hbm.at[t], sem.at[t + 1]))
    for copy in copies:
        copy.start()
    for copy in copies:
        copy.wait()


def shards(section_weights, grad_acc, saved_inputs, cotangent, fresh_grads):
    peers = lax.axis_size("rows")
    cycle = lax.axis_size("blk")
    ticks, _, height, ch, cols = saved_inputs.shape
    bits = peers.bit_length() - 1
    slab = ch // peers
    scale = float(peers * height * cols) ** (-0.5)
    weights = section_weights.transpose(0, 2, 1, 3)
    held = grad_acc.transpose(0, 2, 1, 3)
    anywhere = pl.BlockSpec(memory_space=pl.ANY)
    dma = pltpu.SemaphoreType.DMA
    states, out = pl.pallas_call(
        functools.partial(kernel, (peers, cycle, height, ch, cols, scale)),
        out_shape=(
            pltpu.VMEM(saved_inputs.shape, BF16),
            pltpu.VMEM(held.shape, BF16),
        ),
        in_specs=[anywhere] * 5,
        out_specs=(pl.BlockSpec(memory_space=pltpu.VMEM), pl.BlockSpec(memory_space=pltpu.VMEM)),
        scratch_shapes=[
            pltpu.VMEM((ticks, 9, ch, ch), BF16),
            pltpu.VMEM((ch, 9 * ch), BF16),
            pltpu.VMEM((ticks, height, ch, cols), BF16),
            pltpu.VMEM((ticks, height, ch, cols), BF16),
            pltpu.VMEM((ticks - 1, height, ch, cols), BF16),
            pltpu.VMEM((ch, height * cols), BF16),
            pltpu.VMEM(((height + 2) * 3 * ch, cols), BF16),
            pltpu.VMEM((ticks, 2, ch, cols), BF16),
            pltpu.VMEM((ticks, 3, peers, 3, slab, ch), BF16),
            pltpu.VMEM((2, 3, peers, 3, slab, ch), BF16),
            pltpu.VMEM((2, 3, peers, 3, slab, ch), BF16),
            pltpu.VMEM((3, peers, 3, slab, ch), BF16),
            pltpu.VMEM((2, 9, slab, ch), BF16),
            pltpu.VMEM((9, slab, ch), BF16),
            pltpu.VMEM((3, peers, 3, slab, ch), BF16),
            dma((7,)),
            dma((ticks, 2)),
            dma((ticks, 2)),
            dma((ticks - 1,)),
            dma((ticks - 1,)),
            dma((2, 3, bits)),
            dma((2, 3, bits)),
            dma,
            dma,
            dma((3,)),
            dma((3,)),
            dma((3,)),
            dma((3,)),
        ],
        compiler_params=pltpu.CompilerParams(collective_id=0, has_side_effects=True),
    )(weights, held, saved_inputs, cotangent, fresh_grads)
    states = pltpu.with_memory_space_constraint(states, pltpu.VMEM)
    out = pltpu.with_memory_space_constraint(out, pltpu.VMEM)
    vmem = pl.BlockSpec(memory_space=pltpu.VMEM)
    states, out = pl.pallas_call(
        store,
        out_shape=(
            jax.ShapeDtypeStruct(saved_inputs.shape, BF16),
            jax.ShapeDtypeStruct(held.shape, BF16),
        ),
        in_specs=[vmem, vmem],
        out_specs=(anywhere, anywhere),
        scratch_shapes=[dma((ticks + 1,))],
    )(states, out)
    return states, out.transpose(0, 2, 1, 3)


def solution(mesh):
    return jax.shard_map(
        shards,
        mesh=mesh,
        in_specs=(
            P("blk", None, None, None),
            P("blk", "rows", None, None),
            P(None, "blk", "rows", None, None),
            P("blk", "rows", None, None),
            P(None, "rows", None, None),
        ),
        out_specs=(P(None, "blk", "rows", None, None), P("blk", "rows", None, None)),
        check_vma=False,
    )
```

```python
import functools

import jax
import jax.numpy as jnp
from jax import lax
from jax.experimental import pallas as pl
from jax.experimental.pallas import tpu as pltpu
from jax.sharding import PartitionSpec as P

TICKS = 3
MESH = pl.DeviceIdType.MESH
F32 = jnp.float32
BF16 = jnp.bfloat16


LATE = {(0, 0): (0, 1, 2), (0, 1): (0, 1, 2), (1, 0): (2,), (1, 1): (2,)}
EARLY = (1, 0)
TURN = (2, 0)


def halving(bits, t, core, a):
    return [*range(1, bits), 0] if a in LATE[t, core] else list(range(bits))


def place(bits, t, core, a, value):
    return sum(((value >> k) & 1) << (bits - 1 - at) for at, k in enumerate(halving(bits, t, core, a)))


def kernel(
    shape, w_hbm, acc_hbm, saved_hbm, cot_hbm, fresh_hbm, states, out_ref,
    kern, kern_t, sv, cur, fresh, xs, gs, halo, dk, rx, part, sib, held, held_rx, early,
    load_sem, halo_send, halo_recv, k_send, k_recv, rs_send, rs_recv, acc_send, acc_recv, sib_send, sib_recv, early_send, early_recv,
):
    peers, cycle, height, ch, cols, scale = shape
    bits = peers.bit_length() - 1
    row = lax.axis_index("rows")
    pos = lax.axis_index("blk")
    below = lax.rem(pos + cycle - 1, cycle)
    bit = [lax.rem(row // (1 << k), 2) for k in range(bits)]
    mate = [row + (1 - 2 * bit[k]) * (1 << k) for k in range(bits)]
    has_up = row > 0
    has_down = row < peers - 1
    restart = [None] + [pos == (cycle - t) % cycle for t in range(1, TICKS)]

    loads = [
        pltpu.make_async_copy(cot_hbm.at[0], cur.at[0], load_sem.at[0]),
        pltpu.make_async_copy(saved_hbm.at[0, 0], sv.at[0], load_sem.at[1]),
        pltpu.make_async_copy(w_hbm.at[0], kern.at[0], load_sem.at[2]),
        pltpu.make_async_copy(fresh_hbm, fresh, load_sem.at[3]),
        pltpu.make_async_copy(saved_hbm.at[1, 0], sv.at[1], load_sem.at[4]),
        pltpu.make_async_copy(saved_hbm.at[2, 0], sv.at[2], load_sem.at[5]),
        pltpu.make_async_copy(acc_hbm.at[0], held.at[0], load_sem.at[6]),
    ]
    for load in loads:
        load.start()

    barrier = pltpu.get_barrier_semaphore()
    core = lax.rem(pos, 2)
    sibling = pos + 1 - 2 * core
    far = lax.rem(pos + cycle - (TICKS - 1), cycle)
    hops = sorted({d % cycle for d in (1, -1, TICKS - 1, 1 - TICKS)})
    greet = [{"blk": lax.rem(pos + d, cycle)} for d in hops] + [{"rows": m} for m in mate]
    for who in greet:
        pl.semaphore_signal(barrier, inc=1, device_id=who, device_id_type=MESH)

    other = row + 2 * bit[0] - 1
    has_other = jnp.logical_and(other >= 0, other < peers)

    @pl.when(has_other)
    def _():
        pl.semaphore_signal(barrier, inc=1, device_id={"rows": other}, device_id_type=MESH)

    pl.semaphore_wait(barrier, len(greet) + has_other.astype(jnp.int32))

    def halo_copy(t, side):
        edge = 0 if side == 1 else height - 1
        return pltpu.make_async_remote_copy(
            src_ref=cur.at[t, edge],
            dst_ref=halo.at[t, side],
            send_sem=halo_send.at[t, side],
            recv_sem=halo_recv.at[t, side],
            device_id={"rows": row - 1 if side == 1 else row + 1},
            device_id_type=MESH,
        )

    def halo_start(t):
        @pl.when(jnp.logical_and(has_down, bit[0] == 1))
        def _():
            halo_copy(t, 0).start()

        @pl.when(has_up)
        def _():
            halo_copy(t, 1).start()

        @pl.when(jnp.logical_and(has_down, bit[0] == 0))
        def _():
            halo_copy(t, 0).start()

    def kern_copy(t):
        return pltpu.make_async_remote_copy(
            src_ref=kern.at[t],
            dst_ref=kern.at[t + 1],
            send_sem=k_send.at[t],
            recv_sem=k_recv.at[t],
            device_id={"blk": below},
            device_id_type=MESH,
        )

    held_copy = pltpu.make_async_remote_copy(
        src_ref=held.at[1],
        dst_ref=held_rx,
        send_sem=acc_send,
        recv_sem=acc_recv,
        device_id={"blk": far},
        device_id_type=MESH,
    )

    def sib_copy(a):
        return pltpu.make_async_remote_copy(
            src_ref=dk.at[1, a],
            dst_ref=sib.at[a],
            send_sem=sib_send.at[a],
            recv_sem=sib_recv.at[a],
            device_id={"blk": sibling},
            device_id_type=MESH,
        )

    def early_copy(a):
        return pltpu.make_async_remote_copy(
            src_ref=dk.at[0, a],
            dst_ref=early.at[a],
            send_sem=early_send.at[a],
            recv_sem=early_recv.at[a],
            device_id={"blk": far},
            device_id_type=MESH,
        )

    wide = 3 * ch
    lane = lax.broadcasted_iota(jnp.int32, (ch, cols), 1)

    def put_row(index, value):
        base = pl.multiple_of(index * wide, wide)
        full = value.astype(F32)
        left = jnp.where(lane == cols - 1, 0.0, pltpu.roll(full, cols - 1, 1))
        right = jnp.where(lane == 0, 0.0, pltpu.roll(full, 1, 1))
        gs[pl.ds(base, ch), :] = left.astype(BF16)
        gs[pl.ds(base + ch, ch), :] = value
        gs[pl.ds(base + 2 * ch, ch), :] = right.astype(BF16)

    def inner_rows(t):
        def step(r, carry):
            put_row(r + 1, cur[t, r])
            return carry

        lax.fori_loop(0, height, step, 0)
        for r in range(height):
            xs[:, r * cols : (r + 1) * cols] = jnp.maximum(sv[t, r], 0)

    def outer_rows(t):
        for side, have, index in ((0, has_up, 0), (1, has_down, height + 1)):
            @pl.when(have)
            def _():
                halo_copy(t, side).wait_recv()
                put_row(index, halo[t, side])

            @pl.when(jnp.logical_not(have))
            def _():
                gs[index * wide : (index + 1) * wide, :] = jnp.zeros((wide, cols), BF16)

    def turn_kernel(t):
        for tap in range(9):
            a, b = tap // 3, tap % 3
            at = (2 - a) * wide + b * ch
            kern_t[:, at : at + ch] = kern[t, tap].T

    def back_row(t, r):
        base = pl.multiple_of(r * wide, wide)
        total = jnp.dot(kern_t[...], gs[pl.ds(base, 3 * wide), :], preferred_element_type=F32)
        value = jnp.where(sv[t, r].astype(F32) > 0, total, 0.0).astype(BF16)
        states[t, 0, r] = value
        if t + 1 < TICKS:
            cur[t + 1, r] = jnp.where(restart[t + 1], fresh[t, r], value)

    def back_edges(t):
        def outer(i, carry):
            back_row(t, i * (height - 1))
            return carry

        lax.fori_loop(0, 2, outer, 0)
        if t + 1 < TICKS:
            halo_start(t + 1)

    def back_rest(t):
        def inner(i, carry):
            back_row(t, i + 1)
            return carry

        lax.fori_loop(0, height - 2, inner, 0)

    def back(t):
        back_edges(t)
        back_rest(t)

    slab = ch // peers

    odd_slot = ((0, 1), (1, 0), (1, 1))

    def even_slot(t, a):
        return ((1, 0) if a in EARLY else (0, 0), (0, 1), (1, 0))[t]

    def pick(even, odd):
        return even if even == odd else even + core * (odd - even)

    def along(values, t, a, k):
        even, odd = halving(bits, t, 0, a)[k], halving(bits, t, 1, a)[k]
        return values[even] if even == odd else values[even] + core * (values[odd] - values[even])

    def weight_rows(t, a):
        left = jnp.concatenate(
            [gs[(r + 2 - a) * wide : (r + 3 - a) * wide, :] for r in range(height)], axis=1
        )
        total = lax.dot_general(left, xs[...], (((1,), (1,)), ((), ())), preferred_element_type=F32)
        total = total * scale
        for b in range(3):
            for j in range(peers):
                at = b * ch + j * slab
                value = total[at : at + slab, :]
                at = pick(place(bits, *even_slot(t, a), a, j), place(bits, *odd_slot[t], a, j))
                if t == TICKS - 1:
                    extra = sib[a, at, b].astype(F32)
                    if a in EARLY:
                        extra = extra + early[a, at, b].astype(F32)
                    value = value + jnp.where(core == 0, extra, 0.0)
                dk[t, a, at, b] = value.astype(BF16)

    def add_sibling(a):
        def step(j, carry):
            dk[0, a, j] = (dk[0, a, j].astype(F32) + sib[a, j].astype(F32)).astype(BF16)
            return carry

        lax.fori_loop(0, peers, step, 0)

    def rs_copy(t, a, k):
        count = peers >> (k + 1)
        source = dk.at[2 * t, a] if k == 0 else part.at[t, a, pl.ds(peers - (peers >> (k - 1)), peers >> k)]
        return pltpu.make_async_remote_copy(
            src_ref=source.at[pl.ds((1 - along(bit, t, a, k)) * count, count)],
            dst_ref=rx.at[t, a, pl.ds(peers - (peers >> k), count)],
            send_sem=rs_send.at[t, a, k],
            recv_sem=rs_recv.at[t, a, k],
            device_id={"rows": along(mate, t, a, k)},
            device_id_type=MESH,
        )

    def summed(t, a, k):
        count = peers >> (k + 1)
        rs_copy(t, a, k).wait_recv()
        at = along(bit, t, a, k) * count
        if k == 0:
            own = dk[2 * t, a, pl.ds(at, count)]
        else:
            own = part[t, a, pl.ds(at + peers - (peers >> (k - 1)), count)]
        return own.astype(F32) + rx[t, a, pl.ds(peers - (peers >> k), count)].astype(F32)

    def rs_step(t, a, k):
        count = peers >> (k + 1)
        part[t, a, pl.ds(peers - (peers >> k), count)] = summed(t, a, k).astype(BF16)
        rs_copy(t, a, k + 1).start()

    def rs_last(t, a):
        total = summed(t, a, bits - 1)[0]
        before = held[0, 3 * a : 3 * a + 3] if t == 0 else held_rx[3 * a : 3 * a + 3]
        value = (before.astype(F32) + total).astype(BF16)
        if t == 0:
            held[1, 3 * a : 3 * a + 3] = value
        else:
            out_ref[0, 3 * a : 3 * a + 3] = value

    order = (1, 0, 2)

    first = core == 0
    second = core == 1

    def launch(a):
        @pl.when(first)
        def _():
            if a in EARLY:
                early_copy(a).start()
            else:
                rs_copy(0, a, 0).start()

    rest = [a for a in order if a not in EARLY]

    loads[0].wait()
    halo_start(0)
    loads[2].wait()
    kern_copy(0).start()
    turn_kernel(0)
    loads[1].wait()
    inner_rows(0)
    weight_rows(0, 1)
    launch(1)
    loads[3].wait()
    outer_rows(0)
    back_edges(0)
    for a in (0, 2):
        weight_rows(0, a)
        launch(a)

    @pl.when(first)
    def _():
        kern_copy(0).wait_recv()
        kern_copy(1).start()

    back_rest(0)
    loads[4].wait()
    inner_rows(1)
    weight_rows(1, 1)
    sib_copy(1).start()
    outer_rows(1)

    @pl.when(first)
    def _():
        turn_kernel(1)
        back_edges(1)

    for a in (0, 2):
        weight_rows(1, a)
        sib_copy(a).start()

    sib_copy(1).wait_recv()

    @pl.when(first)
    def _():
        for a in rest:
            rs_step(0, a, 0)

    @pl.when(second)
    def _():
        add_sibling(1)
        rs_copy(0, 1, 0).start()
        kern_copy(0).wait_recv()
        kern_copy(1).start()
        turn_kernel(1)
        back_edges(1)

    for a in (0, 2):
        sib_copy(a).wait_recv()

        @pl.when(second)
        def _():
            add_sibling(a)
            rs_copy(0, a, 0).start()

    back_rest(1)
    loads[5].wait()
    loads[6].wait()
    inner_rows(2)

    def last_rows(a):
        if a in EARLY:
            @pl.when(first)
            def _():
                early_copy(a).wait_recv()

        weight_rows(2, a)
        rs_copy(1, a, 0).start()

    last_rows(1)

    @pl.when(first)
    def _():
        for k in range(1, bits - 1):
            for a in rest:
                rs_step(0, a, k)

    @pl.when(second)
    def _():
        rs_step(0, 1, 0)

    outer_rows(2)
    @pl.when(first)
    def _():
        kern_copy(1).wait_recv()
        turn_kernel(2)

    for a in (0, 2):
        last_rows(a)

    @pl.when(first)
    def _():
        back(2)
        rs_step(1, 1, 0)

    @pl.when(second)
    def _():
        for k in range(1, bits - 1):
            rs_step(0, 1, k)
        rs_step(0, 0, 0)
        rs_step(0, 2, 0)
        rs_step(1, 1, 0)
        for k in range(1, bits - 1):
            rs_step(0, 0, k)
            rs_step(0, 2, k)

    for a in TURN:
        rs_step(1, a, 0)
    for k in range(1, bits - 1):
        rs_step(1, 1, k)

    @pl.when(first)
    def _():
        for a in EARLY:
            held[1, 3 * a : 3 * a + 3] = held[0, 3 * a : 3 * a + 3]
        for a in rest:
            rs_last(0, a)

    @pl.when(second)
    def _():
        for a in order:
            rs_last(0, a)

    held_copy.start()

    for k in range(1, bits - 1):
        for a in TURN:
            rs_step(1, a, k)

    @pl.when(second)
    def _():
        kern_copy(1).wait_recv()
        turn_kernel(2)
        back(2)

    held_copy.wait_recv()
    for a in (1, *TURN):
        rs_last(1, a)

    for t in range(TICKS):
        @pl.when(has_up)
        def _():
            halo_copy(t, 1).wait_send()

        @pl.when(has_down)
        def _():
            halo_copy(t, 0).wait_send()

    for t in range(TICKS - 1):
        kern_copy(t).wait_send()
    for a in range(3):
        sib_copy(a).wait_send()
        for k in range(bits):
            rs_copy(1, a, k).wait_send()
    held_copy.wait_send()

    @pl.when(first)
    def _():
        for a in range(3):
            if a in EARLY:
                early_copy(a).wait_send()
            else:
                for k in range(bits):
                    rs_copy(0, a, k).wait_send()

    @pl.when(second)
    def _():
        for a in range(3):
            for k in range(bits):
                rs_copy(0, a, k).wait_send()


def store(states, out, states_hbm, out_hbm, sem):
    copies = [pltpu.make_async_copy(out, out_hbm, sem.at[0])]
    for t in range(TICKS):
        copies.append(pltpu.make_async_copy(states.at[t], states_hbm.at[t], sem.at[t + 1]))
    for copy in copies:
        copy.start()
    for copy in copies:
        copy.wait()


def shards(section_weights, grad_acc, saved_inputs, cotangent, fresh_grads):
    peers = lax.axis_size("rows")
    cycle = lax.axis_size("blk")
    ticks, _, height, ch, cols = saved_inputs.shape
    bits = peers.bit_length() - 1
    slab = ch // peers
    scale = float(peers * height * cols) ** (-0.5)
    weights = section_weights.transpose(0, 2, 1, 3)
    held = grad_acc.transpose(0, 2, 1, 3)
    anywhere = pl.BlockSpec(memory_space=pl.ANY)
    dma = pltpu.SemaphoreType.DMA
    states, out = pl.pallas_call(
        functools.partial(kernel, (peers, cycle, height, ch, cols, scale)),
        out_shape=(
            pltpu.VMEM(saved_inputs.shape, BF16),
            pltpu.VMEM(held.shape, BF16),
        ),
        in_specs=[anywhere] * 5,
        out_specs=(pl.BlockSpec(memory_space=pltpu.VMEM), pl.BlockSpec(memory_space=pltpu.VMEM)),
        scratch_shapes=[
            pltpu.VMEM((ticks, 9, ch, ch), BF16),
            pltpu.VMEM((ch, 9 * ch), BF16),
            pltpu.VMEM((ticks, height, ch, cols), BF16),
            pltpu.VMEM((ticks, height, ch, cols), BF16),
            pltpu.VMEM((ticks - 1, height, ch, cols), BF16),
            pltpu.VMEM((ch, height * cols), BF16),
            pltpu.VMEM(((height + 2) * 3 * ch, cols), BF16),
            pltpu.VMEM((ticks, 2, ch, cols), BF16),
            pltpu.VMEM((ticks, 3, peers, 3, slab, ch), BF16),
            pltpu.VMEM((2, 3, peers, 3, slab, ch), BF16),
            pltpu.VMEM((2, 3, peers, 3, slab, ch), BF16),
            pltpu.VMEM((3, peers, 3, slab, ch), BF16),
            pltpu.VMEM((2, 9, slab, ch), BF16),
            pltpu.VMEM((9, slab, ch), BF16),
            pltpu.VMEM((3, peers, 3, slab, ch), BF16),
            dma((7,)),
            dma((ticks, 2)),
            dma((ticks, 2)),
            dma((ticks - 1,)),
            dma((ticks - 1,)),
            dma((2, 3, bits)),
            dma((2, 3, bits)),
            dma,
            dma,
            dma((3,)),
            dma((3,)),
            dma((3,)),
            dma((3,)),
        ],
        compiler_params=pltpu.CompilerParams(collective_id=0, has_side_effects=True),
    )(weights, held, saved_inputs, cotangent, fresh_grads)
    states = pltpu.with_memory_space_constraint(states, pltpu.VMEM)
    out = pltpu.with_memory_space_constraint(out, pltpu.VMEM)
    vmem = pl.BlockSpec(memory_space=pltpu.VMEM)
    states, out = pl.pallas_call(
        store,
        out_shape=(
            jax.ShapeDtypeStruct(saved_inputs.shape, BF16),
            jax.ShapeDtypeStruct(held.shape, BF16),
        ),
        in_specs=[vmem, vmem],
        out_specs=(anywhere, anywhere),
        scratch_shapes=[dma((ticks + 1,))],
    )(states, out)
    return states, out.transpose(0, 2, 1, 3)


def solution(mesh):
    return jax.shard_map(
        shards,
        mesh=mesh,
        in_specs=(
            P("blk", None, None, None),
            P("blk", "rows", None, None),
            P(None, "blk", "rows", None, None),
            P("blk", "rows", None, None),
            P(None, "rows", None, None),
        ),
        out_specs=(P(None, "blk", "rows", None, None), P("blk", "rows", None, None)),
        check_vma=False,
    )
```
